256 devices in a mesh: ma: 64 (over x, z, core), row: 4 (over y).
Axes of the slice: x: 4, y: 4, z: 8, core: 2. Of those that a mesh axis runs over, the one named last changes fastest.
Arguments:
- fields: bfloat16 [6, 64, 2, 512, 512], P(None, 'row', None, 'ma'), may hold values from -6 to 6
- legendre: bfloat16 [512, 512, 768], P('ma'), may hold values from -0.25 to 0.25
- quad: float32 [768], replicated, may hold values from 0.1 to 1.9
- assign: int32 [512], replicated, may hold values from 0 to 511, each once
Outputs:
- induction: float32 [3, 64, 2, 512, 512], P(None, 'row', None, 'ma')
The draws below stay inside these ranges and needn't reach their ends.
Inputs may be any that keep to these rules, and one draw needn't show every extreme that they name: assign holds each order 0 to 511 exactly once; order slot s of fields, legendre and induction belongs to order assign[s].
All inputs are finite; a program needn't handle non-finite values.
Results may differ from the reference program's by a relative error of at most 0.0068.
Values may be sent and summed in bfloat16 or wider, within the bound.
A program may use at most 128 MiB of HBM per device.

```python
import math
import jax
import jax.numpy as jnp
from jax import lax

L = 512
M = 512
NLAT = 768
NLON = 1536
NR = 64


def level_of(rng, extent, cuts, low, top_value):
    def one(position, blocks):
        draws = jax.random.uniform(jax.random.fold_in(jax.random.fold_in(rng, 6), position), (blocks,), jnp.float32, low / len(cuts), top_value / len(cuts))
        return jnp.repeat(jnp.exp(draws), extent[position] // blocks).reshape((-1,) + (1,) * (len(extent) - position - 1))

    loudness = one(*cuts[0])
    for cut in cuts[1:]:
        loudness = loudness * one(*cut)
    return loudness


def centred(rng, dims, width, most, pieces=(), held_as=jnp.bfloat16):
    array = width * jax.random.normal(rng, dims, jnp.float32)
    if pieces:
        array = array * level_of(rng, dims, pieces, -0.22, 0.18)
    return jnp.clip(array, -most, most).astype(held_as)


def setup_inputs(seed: int = 0) -> dict:
    key_of = jax.random.split(jax.random.key(seed), 5)
    fields = centred(key_of[0], (6, NR, 2, M, L), 1.0, 6.0, ((1, 4), (3, 64)))
    legendre = centred(key_of[1], (M, L, NLAT), L ** -0.5, 0.25, ((0, 64),))
    quad = jnp.clip(1.0 + 0.18 * jax.random.normal(key_of[2], (NLAT,), jnp.float32), 0.1, 1.9)
    assign = jax.random.permutation(key_of[3], M).astype(jnp.int32)
    return dict(fields=fields, legendre=legendre, quad=quad, assign=assign)


def longitude_tables(assign, lon_count):
    order_vals = assign.astype(jnp.int32)
    lon_index = jnp.arange(lon_count, dtype=jnp.int32)
    phase_angle = (order_vals[:, None] * lon_index[None, :] % lon_count).astype(jnp.float32) * (2.0 * math.pi / lon_count)
    order_total = assign.shape[0]
    factor = jnp.where(order_vals > 0, 2.0, 1.0).astype(jnp.float32) / math.sqrt(order_total)
    cosine = jnp.cos(phase_angle)
    sine_part = jnp.sin(phase_angle)
    synth_table = jnp.stack([factor[:, None] * cosine, -factor[:, None] * sine_part]).astype(jnp.bfloat16)
    analysis_table = (jnp.stack([cosine, -sine_part]) / math.sqrt(lon_count)).astype(jnp.bfloat16)
    return (synth_table, analysis_table)

def reference(fields, legendre, quad, assign):
    order_total = assign.shape[0]
    degrees = legendre.shape[1]
    lat_count = legendre.shape[2]
    level_total = fields.shape[1]
    keep_mask = (jnp.arange(degrees, dtype=jnp.int32)[None, :] >= assign[:, None]).astype(jnp.bfloat16)
    synth_table, analysis_table = longitude_tables(assign, NLON)
    row_count = 6 * level_total * 2

    def inverse(slot_index):
        coefficient = lax.dynamic_index_in_dim(fields, slot_index, 3, keepdims=False)
        coefficient = coefficient * lax.dynamic_index_in_dim(keep_mask, slot_index, 0, keepdims=False)
        table_here = lax.dynamic_index_in_dim(legendre, slot_index, 0, keepdims=False)
        values = jnp.dot(coefficient.reshape(row_count, degrees), table_here, preferred_element_type=jnp.float32)
        return values.astype(jnp.bfloat16).reshape(6, level_total, 2, lat_count)
    spat = lax.map(inverse, jnp.arange(order_total, dtype=jnp.int32))
    radius = 0.5 + (jnp.arange(level_total).astype(jnp.float32) + 0.5) / level_total
    flat_synth = synth_table.reshape(2 * order_total, NLON)
    flat_analysis = analysis_table.reshape(2 * order_total, NLON)

    def physical(level):
        level_block = lax.dynamic_index_in_dim(spat, level, 2, keepdims=False)
        level_block = jnp.transpose(level_block, (1, 2, 0, 3)).reshape(6, 2 * order_total, lat_count)
        components = [jnp.dot(level_block[field_index].T, flat_synth, preferred_element_type=jnp.float32) for field_index in range(6)]
        vel_r, vel_t, vel_p, mag_r, mag_t, mag_p = components
        emf_radial = vel_t * mag_p - vel_p * mag_t
        emf_theta = vel_p * mag_r - vel_r * mag_p
        emf_phi = vel_r * mag_t - vel_t * mag_r
        radius_here = radius[level]
        return (emf_radial.astype(jnp.bfloat16), (radius_here * emf_theta).astype(jnp.bfloat16), (radius_here * emf_phi).astype(jnp.bfloat16))
    emf_radial_all, scaled_theta, scaled_phi = lax.map(physical, jnp.arange(level_total, dtype=jnp.int32))
    zero_level = jnp.zeros((1, lat_count, NLON), jnp.bfloat16)
    padded_theta = jnp.concatenate([zero_level, scaled_theta, zero_level], axis=0)
    padded_phi = jnp.concatenate([zero_level, scaled_phi, zero_level], axis=0)

    def spectral(level):

        def radial_diff(padded):
            below_level = lax.dynamic_index_in_dim(padded, level, 0, keepdims=False).astype(jnp.float32)
            middle = lax.dynamic_index_in_dim(padded, level + 1, 0, keepdims=False).astype(jnp.float32)
            above_level = lax.dynamic_index_in_dim(padded, level + 2, 0, keepdims=False).astype(jnp.float32)
            return jnp.where(level == 0, above_level - middle, jnp.where(level == level_total - 1, middle - below_level, 0.5 * (above_level - below_level)))
        radius_here = radius[level]
        curl_theta = (-radial_diff(padded_phi) / radius_here).astype(jnp.bfloat16)
        curl_phi = (radial_diff(padded_theta) / radius_here).astype(jnp.bfloat16)
        emf_here = lax.dynamic_index_in_dim(emf_radial_all, level, 0, keepdims=False)
        results = []
        for term in (emf_here, curl_theta, curl_phi):
            longitude_coef = jnp.dot(term, flat_analysis.T, preferred_element_type=jnp.float32)
            results.append((longitude_coef * quad[:, None]).astype(jnp.bfloat16))
        return jnp.stack(results)
    weighted = lax.map(spectral, jnp.arange(level_total, dtype=jnp.int32))
    weighted = weighted.reshape(level_total, 3, lat_count, 2, order_total)

    def forward(slot_index):
        exchanged = lax.dynamic_index_in_dim(weighted, slot_index, 4, keepdims=False)
        exchanged = jnp.transpose(exchanged, (0, 1, 3, 2)).reshape(level_total * 6, lat_count)
        table_here = lax.dynamic_index_in_dim(legendre, slot_index, 0, keepdims=False)
        values = jnp.dot(exchanged, table_here.T, preferred_element_type=jnp.float32)
        values = values * lax.dynamic_index_in_dim(keep_mask, slot_index, 0, keepdims=False).astype(jnp.float32)
        return values.reshape(level_total, 3, 2, degrees)
    result = lax.map(forward, jnp.arange(order_total, dtype=jnp.int32))
    return jnp.transpose(result, (2, 1, 3, 0, 4))
```

```python
import functools
import math

import jax
import jax.numpy as jnp
from jax import lax
from jax.experimental import pallas as pl
from jax.experimental.pallas import tpu as pltpu
from jax.sharding import PartitionSpec as P

NLON = 1536
F32 = jnp.float32
BF16 = jnp.bfloat16


def left_lanes(rows):
    return lax.broadcasted_iota(jnp.int32, (rows, 128), 1) < 64


def inverse_kernel(orders_ref, fields_ref, leg_ref, out_ref, coef, spat):
    s = pl.program_id(0)

    @pl.when(s == 0)
    def _():
        for t in range(4):
            coef[t] = fields_ref[:, t * 128 : t * 128 + 128].astype(F32)

    x = jnp.concatenate([coef[t, pl.ds(s, 192, stride=8), :] for t in range(4)], axis=1)
    degree = lax.broadcasted_iota(jnp.int32, x.shape, 1)
    x = jnp.where(degree >= orders_ref[s], x, 0.0).astype(BF16)
    y = jnp.dot(x, leg_ref[0], preferred_element_type=F32)
    for t in range(6):
        spat[t, pl.ds(s, 192, stride=8), :] = y[:, t * 128 : t * 128 + 128]

    @pl.when(s == 7)
    def _():
        left = left_lanes(16)

        def level(k, carry):
            for jq in range(4):
                base, odd = 3 * (jq // 2), jq % 2
                for q in range(3):
                    tile = base + odd if q < 2 else base + 2
                    high = q == 1 or (q == 2 and odd)
                    for p in range(3):
                        u = spat[tile, pl.ds(pl.multiple_of(p * 256 + k * 16, 16), 16), :]
                        b = spat[tile, pl.ds(pl.multiple_of(p * 256 + 768 + k * 16, 16), 16), :]
                        if high:
                            v = jnp.where(left, pltpu.roll(u, 64, 1), b)
                        else:
                            v = jnp.where(left, u, pltpu.roll(b, 64, 1))
                        at = (q * 3 + p) * 128
                        out_ref[k * 4 + jq, :, at : at + 128] = v.astype(BF16)
            return carry

        lax.fori_loop(0, 16, level, 0)


def inverse(orders, fields, legendre):
    return pl.pallas_call(
        inverse_kernel,
        grid_spec=pltpu.PrefetchScalarGridSpec(
            num_scalar_prefetch=1,
            grid=(8,),
            in_specs=[
                pl.BlockSpec((1536, 512), lambda s, o: (0, 0)),
                pl.BlockSpec((1, 512, 768), lambda s, o: (s, 0, 0)),
            ],
            out_specs=pl.BlockSpec((64, 16, 1152), lambda s, o: (0, 0, 0)),
            scratch_shapes=[pltpu.VMEM((4, 1536, 128), F32), pltpu.VMEM((6, 1536, 128), F32)],
        ),
        out_shape=jax.ShapeDtypeStruct((64, 16, 1152), BF16),
        name="inverse",
    )(orders, fields, legendre)


def grid_kernel(radius_ref, got_ref, synth_ref, analysis_ref, quad_ref, out_ref, emf):
    radius = radius_ref[0]
    tile_rows = 256
    left = left_lanes(tile_rows)

    def synth(i, carry):
        rows = pl.ds(pl.multiple_of(i * tile_rows, tile_rows), tile_rows)
        lines = synth_ref[rows, :]
        diffs = []
        for q in range(3):
            g = jnp.dot(
                lines, got_ref[:, q * 384 : q * 384 + 384], preferred_element_type=F32
            )
            c = [g[:, p * 128 : p * 128 + 128] for p in range(3)]
            r = [pltpu.roll(v, 64, 1) for v in c]
            d = []
            for a, b in ((1, 2), (2, 0), (0, 1)):
                t = c[a] * r[b]
                d.append(t - pltpu.roll(t, 64, 1))
            diffs.append([d[0], d[1] * radius, d[2] * radius])
        for g in range(3):
            emf[rows, g * 128 : g * 128 + 128] = jnp.where(
                left, diffs[0][g], -diffs[1][g]
            ).astype(BF16)
        emf[rows, 384:512] = jnp.where(left, diffs[2][0], -diffs[2][1]).astype(BF16)
        emf[rows, 512:640] = diffs[2][2].astype(BF16)
        return carry

    lax.fori_loop(0, NLON // tile_rows, synth, 0)

    def analyse(i, carry):
        rows = pl.ds(pl.multiple_of(i * tile_rows, tile_rows), tile_rows)
        w = jnp.dot(analysis_ref[rows, :], emf[...], preferred_element_type=F32)
        w = w * quad_ref[...]
        dests = pl.ds(i * (tile_rows // 16), tile_rows // 16)
        for t in range(4):
            block = w[:, t * 128 : t * 128 + 128].reshape(tile_rows // 16, 16, 128)
            out_ref[dests, t * 16 : t * 16 + 16, :] = block.astype(BF16)
        last = w[:, 512:640].reshape(tile_rows // 16, 16, 128)
        lane = lax.broadcasted_iota(jnp.int32, (tile_rows // 16, 8, 128), 2)
        pair = jnp.where(lane < 64, last[:, :8], -last[:, 8:])
        out_ref[dests, 64:72, :] = pair.astype(BF16)
        return carry

    lax.fori_loop(0, 1024 // tile_rows, analyse, 0)


def grid_space(radius, got, synth, analysis, quad_lanes):
    vmem = pl.BlockSpec(memory_space=pltpu.VMEM)
    return pl.pallas_call(
        grid_kernel,
        in_specs=[pl.BlockSpec(memory_space=pltpu.SMEM), vmem, vmem, vmem, vmem],
        out_specs=vmem,
        scratch_shapes=[pltpu.VMEM((NLON, 640), BF16)],
        out_shape=jax.ShapeDtypeStruct((64, 72, 128), BF16),
        name="grid",
    )(radius, got, synth, analysis, quad_lanes)


def forward_kernel(orders_ref, got_ref, low_ref, high_ref, coef_ref, leg_ref, out_ref, full, lhs, done):
    s = pl.program_id(0)

    @pl.when(s == 0)
    def _():
        left = left_lanes(16)
        left8 = left_lanes(8)

        def unpack(block, first, level):
            base = pl.multiple_of(level * 16, 16)
            for pair in range(2):
                ev, od = first + pair * 2, first + pair * 2 + 1
                lanes = [pair * 3 + t for t in range(3)]
                for g in (1, 2):
                    rows = pl.ds(pl.multiple_of((g - 1) * 288 + base, 16), 16)
                    full[lanes[0], rows, :] = block(ev, g * 16, 16)
                    full[lanes[1], rows, :] = block(od, g * 16, 16)
                e, o = block(ev, 48, 16), block(od, 48, 16)
                full[lanes[2], pl.ds(base, 16), :] = jnp.where(
                    left, pltpu.roll(e, 64, 1), o
                )
                e, o = block(ev, 64, 8), block(od, 64, 8)
                full[lanes[2], pl.ds(pl.multiple_of(288 + base, 16), 8), :] = jnp.where(
                    left8, e, pltpu.roll(o, 64, 1)
                )
                full[lanes[2], pl.ds(pl.multiple_of(296 + base, 8), 8), :] = jnp.where(
                    left8, pltpu.roll(e, 64, 1), o
                )

        unpack(lambda i, at, n: low_ref[i, at : at + n, :].astype(F32), 0, 0)
        unpack(lambda i, at, n: high_ref[i, at : at + n, :].astype(F32), 0, 17)

        def level(k, carry):
            block = lambda i, at, n: got_ref[i, at : at + n, :].astype(F32)
            unpack(block, k * 4, k + 1)
            for pair in range(2):
                ev, od = k * 4 + pair * 2, k * 4 + pair * 2 + 1
                rows = pl.ds(pl.multiple_of(k * 16, 16), 16)
                lhs[pair * 3, rows, :] = block(ev, 0, 16)
                lhs[pair * 3 + 1, rows, :] = block(od, 0, 16)
                lhs[pair * 3 + 2, rows, :] = jnp.where(
                    left, block(ev, 48, 16), pltpu.roll(block(od, 48, 16), 64, 1)
                )
            return carry

        lax.fori_loop(0, 16, level, 0)

        def derive(k, carry):
            up, mid, down = coef_ref[0, k], coef_ref[1, k], coef_ref[2, k]

            def diff(at):
                here = lambda n: full[:, pl.ds(pl.multiple_of(at + (k + n) * 16, 16), 16), :]
                return up * here(2) + mid * here(1) + down * here(0)

            lhs[:, pl.ds(pl.multiple_of(256 + k * 16, 16), 16), :] = -diff(288)
            lhs[:, pl.ds(pl.multiple_of(512 + k * 16, 16), 16), :] = diff(0)
            return carry

        lax.fori_loop(0, 16, derive, 0)

    x = jnp.concatenate([lhs[t, pl.ds(s, 96, stride=8), :] for t in range(6)], axis=1)
    x = x.astype(BF16)
    y = lax.dot_general(x, leg_ref[0], (((1,), (1,)), ((), ())), preferred_element_type=F32)
    degree = lax.broadcasted_iota(jnp.int32, y.shape, 1)
    y = jnp.where(degree >= orders_ref[s], y, 0.0)
    for t in range(4):
        done[t, pl.ds(s, 96, stride=8), :] = y[:, t * 128 : t * 128 + 128]

    @pl.when(s == 7)
    def _():
        for t in range(4):
            out_ref[:, t * 128 : t * 128 + 128] = done[t]


def forward(orders, got, low, high, coef, legendre):
    fixed = lambda *shape: pl.BlockSpec(shape, lambda s, o: (0,) * len(shape))
    return pl.pallas_call(
        forward_kernel,
        grid_spec=pltpu.PrefetchScalarGridSpec(
            num_scalar_prefetch=1,
            grid=(8,),
            in_specs=[
                fixed(64, 72, 128),
                fixed(4, 72, 128),
                fixed(4, 72, 128),
                pl.BlockSpec(memory_space=pltpu.SMEM),
                pl.BlockSpec((1, 512, 768), lambda s, o: (s, 0, 0)),
            ],
            out_specs=fixed(768, 512),
            scratch_shapes=[pltpu.VMEM((6, 576, 128), F32), pltpu.VMEM((6, 768, 128), F32), pltpu.VMEM((4, 768, 128), F32)],
        ),
        out_shape=jax.ShapeDtypeStruct((768, 512), F32),
        name="forward",
    )(orders, got, low, high, coef, legendre)


def tables(assign):
    order = jnp.tile(assign.reshape(64, 1, 8), (1, 2, 1)).reshape(1024)
    shift = jnp.tile(jnp.array([0, NLON // 4], jnp.int32)[None, :, None], (64, 1, 8)).reshape(1024)
    lon = jnp.arange(NLON, dtype=jnp.int32)
    factor = jnp.where(order > 0, 2.0, 1.0).astype(F32) / math.sqrt(assign.shape[0])
    step = 2.0 * math.pi / NLON
    down = jnp.cos(((lon[:, None] * order[None, :] + shift[None, :]) % NLON).astype(F32) * step)
    synth = (factor[None, :] * down).astype(BF16)
    across = jnp.cos(((order[:, None] * lon[None, :] + shift[:, None]) % NLON).astype(F32) * step)
    analysis = (across / math.sqrt(NLON)).astype(BF16)
    return synth, analysis


def shards(fields, legendre, quad, assign):
    ma = lax.axis_index("ma")
    row = lax.axis_index("row")
    rows = lax.axis_size("row")
    levels = fields.shape[1]
    total = levels * rows
    orders = lax.dynamic_slice_in_dim(assign, ma * 8, 8)

    packed = inverse(orders, fields.reshape(1536, 512), legendre)
    got = lax.all_to_all(packed, "ma", split_axis=0, concat_axis=0, tiled=True)

    synth, analysis = tables(assign)
    level = row * levels + ma // 4
    radius = 0.5 + (level.astype(F32) + 0.5) / total
    jq = ma % 4
    first = (3 * (jq // 2) + jq % 2) * 128
    second = (3 * (jq // 2) + 2) * 128 + (jq % 2) * 64
    pair = lax.dynamic_slice_in_dim(quad, first, 128)
    half = lax.dynamic_slice_in_dim(quad, second, 64)
    quad_lanes = jnp.concatenate([pair, pair, pair, half, half, half, half])[None, :]

    out = grid_space(radius[None], got.reshape(1024, 1152), synth, analysis, quad_lanes)
    back = lax.all_to_all(out, "ma", split_axis=0, concat_axis=0, tiled=True)

    up = [(i, i + 1) for i in range(rows - 1)]
    down = [(b, a) for a, b in up]
    low = lax.ppermute(back[60:], "row", up)
    high = lax.ppermute(back[:4], "row", down)

    index = row * levels + jnp.arange(levels, dtype=jnp.int32)
    inv = 1.0 / (0.5 + (index.astype(F32) + 0.5) / total)
    bottom, top = index == 0, index == total - 1
    coef = jnp.stack(
        [
            jnp.where(top, 0.0, jnp.where(bottom, 1.0, 0.5)) * inv,
            jnp.where(bottom, -1.0, jnp.where(top, 1.0, 0.0)) * inv,
            jnp.where(bottom, 0.0, jnp.where(top, -1.0, -0.5)) * inv,
        ]
    )
    result = forward(orders, back, low, high, coef, legendre)
    return result.reshape(3, levels, 2, 8, 512)


def solution(mesh):
    return jax.shard_map(
        shards,
        mesh=mesh,
        in_specs=(P(None, "row", None, "ma", None), P("ma", None, None), P(), P()),
        out_specs=P(None, "row", None, "ma", None),
        check_vma=False,
    )
```

```python
import math

import jax
import jax.numpy as jnp
import numpy as np
from jax import lax
from jax.experimental import pallas as pl
from jax.experimental.pallas import tpu as pltpu
from jax.sharding import PartitionSpec as P

NLON = 1536
PEERS = 64
F32 = jnp.float32
BF16 = jnp.bfloat16
MESH = pl.DeviceIdType.MESH


def fit(function, terms):
    z = 0.125 - 0.1251 * np.cos(np.pi * (np.arange(400) + 0.5) / 400)
    z = np.clip(z, 1e-12, None)
    values = function(np.sqrt(z))
    basis = np.polynomial.Chebyshev.fit(z, values, terms - 1, domain=[0.0, 0.25])
    power = basis.convert(kind=np.polynomial.Polynomial)
    return [float(c) for c in power.coef]


COS = fit(lambda t: np.cos(2 * np.pi * t), 9)
SIN = fit(lambda t: np.sin(2 * np.pi * t) / t, 9)


def horner(coefs, z):
    total = jnp.full(z.shape, coefs[-1], F32)
    for c in coefs[-2::-1]:
        total = total * z + c
    return total


def cos_sin(product):
    turns = jnp.floor(product * (1.0 / NLON) + 0.5)
    t = (product - turns * NLON) * (1.0 / NLON)
    z = t * t
    return horner(COS, z), t * horner(SIN, z)


def aligned(value, size):
    return pl.ds(pl.multiple_of(value, size), size)


def kernel(
    assign_ref, lanes_ref, quad_ref, fields_hbm, leg_hbm, out_ref,
    fbuf, coef, xs, leg, spat, send1, recv1, synth, analysis, cb, sb, ca, sa,
    emf, send2, recv2, low, high, full, lhs, done,
    in_sem, ssem1, rsem1, lsem1, ssem2, rsem2, lsem2, hsend, hrecv,
):
    me = lax.axis_index("ma")
    row = lax.axis_index("row")
    rows = lax.axis_size("row")
    above = lax.rem(row + 1, rows)
    below = lax.rem(row + rows - 1, rows)
    total = 16 * rows

    fetch = pltpu.make_async_copy(fields_hbm, fbuf, in_sem.at[8])
    fetch.start()
    fetches = [pltpu.make_async_copy(leg_hbm.at[s], leg.at[s], in_sem.at[s]) for s in range(8)]
    for f in fetches:
        f.start()

    barrier = pltpu.get_barrier_semaphore()

    def greet(i, carry):
        pl.semaphore_signal(
            barrier, inc=1, device_id={"ma": lax.rem(me + i, PEERS)}, device_id_type=MESH
        )
        return carry

    lax.fori_loop(1, PEERS, greet, 0)
    for other in (above, below):
        pl.semaphore_signal(barrier, inc=1, device_id={"row": other}, device_id_type=MESH)

    left = lax.broadcasted_iota(jnp.int32, (16, 128), 1) < 64

    fetch.wait()
    for t in range(4):
        coef[t] = fbuf[:, t * 128 : t * 128 + 128].astype(F32)

    def mask(s, carry):
        order = assign_ref[me * 8 + s]
        for t in range(4):
            x = coef[t, pl.ds(s, 192, stride=8), :]
            degree = lax.broadcasted_iota(jnp.int32, x.shape, 1) + t * 128
            xs[s, :, t * 128 : t * 128 + 128] = jnp.where(degree >= order, x, 0.0).astype(BF16)
        return carry

    lax.fori_loop(0, 8, mask, 0)

    def level_group(i):
        half = (i + 1) // 2
        odd = lax.rem(i, 2)
        return lax.rem(me // 4 + odd * half + (1 - odd) * (16 - half), 16)

    def issue1(q, i):
        k = level_group(i)
        for jq in range(4):
            dest = k * 4 + jq

            @pl.when(dest != me)
            def _():
                pltpu.make_async_remote_copy(
                    src_ref=send1.at[q, dest],
                    dst_ref=recv1.at[q, me],
                    send_sem=ssem1.at[q],
                    recv_sem=rsem1.at[q],
                    device_id={"ma": dest},
                    device_id_type=MESH,
                ).start()

            @pl.when(dest == me)
            def _():
                pltpu.make_async_copy(send1.at[q, dest], recv1.at[q, me], lsem1.at[q]).start()

    for q in range(3):
        for s in range(8):
            if q == 0:
                fetches[s].wait()
            table = jnp.concatenate(
                [leg[s, :, q * 128 : q * 128 + 128], leg[s, :, q * 128 + 384 : q * 128 + 512]],
                axis=1,
            )
            y = jnp.dot(xs[s], table, preferred_element_type=F32)
            spat[0, pl.ds(s, 192, stride=8), :] = y[:, :128]
            spat[1, pl.ds(s, 192, stride=8), :] = y[:, 128:]

        if q == 0:
            pl.semaphore_wait(barrier, PEERS + 1)

        def group(i, carry):
            k = level_group(i)
            for jq in range(4):
                for p in range(3):
                    u = spat[jq // 2, aligned(p * 256 + k * 16, 16), :]
                    b = spat[jq // 2, aligned(p * 256 + 768 + k * 16, 16), :]
                    if jq % 2:
                        v = jnp.where(left, pltpu.roll(u, 64, 1), b)
                    else:
                        v = jnp.where(left, u, pltpu.roll(b, 64, 1))
                    send1[q, k * 4 + jq, :, p * 128 : p * 128 + 128] = v.astype(BF16)

            @pl.when(i > 0)
            def _():
                issue1(q, i - 1)

            return carry

        lax.fori_loop(0, 16, group, 0)
        issue1(q, 15)

    m = lanes_ref[...].astype(F32)
    lane = lax.broadcasted_iota(jnp.int32, (16, 1024), 1)
    second = lax.rem(lane // 8, 2) == 1
    n1 = lax.broadcasted_iota(jnp.int32, (16, 1024), 0).astype(F32) * 128.0
    c, s_ = cos_sin(n1 * m)
    ca[...] = jnp.where(second, -s_, c)
    sa[...] = jnp.where(second, c, s_)

    def fine(i, carry):
        n0 = (lax.broadcasted_iota(jnp.int32, (16, 1024), 0) + i * 16).astype(F32)
        c, s_ = cos_sin(n0 * m)
        cb[aligned(i * 16, 16), :] = c
        sb[aligned(i * 16, 16), :] = s_
        return carry

    lax.fori_loop(0, 8, fine, 0)
    factor = jnp.where(m > 0.0, 2.0, 1.0) * (1.0 / math.sqrt(PEERS * 8))
    for n in range(NLON // 128):
        cn = ca[n : n + 1, :] * factor
        sn = sa[n : n + 1, :] * factor

        def fill(i, carry):
            at = aligned(i * 16, 16)
            synth[aligned(n * 128 + i * 16, 16), :] = (cn * cb[at, :] - sn * sb[at, :]).astype(BF16)
            return carry

        lax.fori_loop(0, 8, fill, 0)

    def across(i, carry):
        at = aligned(i * 128, 128)
        cbt, sbt = cb[:, at].T, sb[:, at].T
        cat, sat = ca[:, at].T, sa[:, at].T
        scale = 1.0 / math.sqrt(NLON)
        cat, sat = cat * scale, sat * scale
        for n in range(NLON // 128):
            v = cat[:, n : n + 1] * cbt - sat[:, n : n + 1] * sbt
            analysis[at, n * 128 : n * 128 + 128] = v.astype(BF16)
        return carry

    lax.fori_loop(0, 8, across, 0)

    jq = lax.rem(me, 4)
    level = row * 16 + me // 4
    radius = 0.5 + (level.astype(F32) + 0.5) * (1.0 / total)
    lane1 = lax.broadcasted_iota(jnp.int32, (1, 128), 1)
    mine = lane1 // 64 == lax.rem(jq, 2)
    left_tall = lax.broadcasted_iota(jnp.int32, (256, 128), 1) < 64

    def issue2(q, i):
        tile = lax.rem(me // 16 + i, 4)

        def one(j, carry):
            dest = tile * 16 + lax.rem(me + j, 16)

            @pl.when(dest != me)
            def _():
                pltpu.make_async_remote_copy(
                    src_ref=send2.at[q, dest],
                    dst_ref=recv2.at[q, me],
                    send_sem=ssem2.at[q],
                    recv_sem=rsem2.at[q],
                    device_id={"ma": dest},
                    device_id_type=MESH,
                ).start()

            @pl.when(dest == me)
            def _():
                pltpu.make_async_copy(send2.at[q, dest], recv2.at[q, me], lsem2.at[q]).start()

            return carry

        lax.fori_loop(0, 16, one, 0)

    for q in range(3):
        span = recv1.at[q, pl.ds(0, PEERS - 1)]
        pltpu.make_async_copy(span, span, rsem1.at[q]).wait()
        pltpu.make_async_copy(recv1.at[q, 0], recv1.at[q, 0], lsem1.at[q]).wait()
        quads = quad_ref[pl.ds((jq // 2) * 3 + q, 1), :]
        quads = jnp.where(mine, quads, pltpu.roll(quads, 64, 1))

        def synthesise(i, carry):
            at = aligned(i * 256, 256)
            got = recv1[q].reshape(1024, 384)
            g = jnp.dot(synth[at, :], got, preferred_element_type=F32)
            c = [g[:, p * 128 : p * 128 + 128] for p in range(3)]
            r = [pltpu.roll(v, 64, 1) for v in c]
            d = []
            for a, b in ((1, 2), (2, 0), (0, 1)):
                t = c[a] * r[b]
                d.append(t - pltpu.roll(t, 64, 1))
            emf[at, 0:128] = jnp.where(left_tall, d[0], -(d[1] * radius)).astype(BF16)
            emf[at, 128:256] = (d[2] * radius).astype(BF16)
            return carry

        lax.fori_loop(0, NLON // 256, synthesise, 0)

        def analyse(i, carry):
            tile = lax.rem(me // 16 + i, 4)
            w = jnp.dot(analysis[aligned(tile * 256, 256), :], emf[...], preferred_element_type=F32)
            dests = aligned(tile * 16, 16)
            send2[q, dests, 0:16, :] = (w[:, :128] * quads).reshape(16, 16, 128).astype(BF16)
            last = (w[:, 128:] * quads).reshape(16, 16, 128)
            lane3 = lax.broadcasted_iota(jnp.int32, (16, 8, 128), 2)
            pair = jnp.where(lane3 < 64, last[:, :8], -last[:, 8:])
            send2[q, dests, 16:24, :] = pair.astype(BF16)

            @pl.when(i > 0)
            def _():
                issue2(q, i - 1)

            return carry

        lax.fori_loop(0, 4, analyse, 0)
        issue2(q, 3)

    left8 = lax.broadcasted_iota(jnp.int32, (8, 128), 1) < 64

    def halos(q):
        up = pltpu.make_async_remote_copy(
            src_ref=recv2.at[q, pl.ds(60, 4)],
            dst_ref=low.at[q],
            send_sem=hsend.at[2 * q],
            recv_sem=hrecv.at[2 * q],
            device_id={"row": above},
            device_id_type=MESH,
        )
        down = pltpu.make_async_remote_copy(
            src_ref=recv2.at[q, pl.ds(0, 4)],
            dst_ref=high.at[q],
            send_sem=hsend.at[2 * q + 1],
            recv_sem=hrecv.at[2 * q + 1],
            device_id={"row": below},
            device_id_type=MESH,
        )
        return up, down

    def unpack(block, first, slot, k):
        base = slot * 16
        for pair in range(2):
            ev, od = first + pair * 2, first + pair * 2 + 1
            e, o = block(ev, 0, 16), block(od, 0, 16)
            if k is not None:
                lhs[pair, aligned(k * 16, 16), :] = jnp.where(left, e, pltpu.roll(o, 64, 1))
            full[pair, aligned(base, 16), :] = jnp.where(left, pltpu.roll(e, 64, 1), o)
            e, o = block(ev, 16, 8), block(od, 16, 8)
            full[pair, aligned(288 + base, 8), :] = jnp.where(left8, e, pltpu.roll(o, 64, 1))
            full[pair, aligned(296 + base, 8), :] = jnp.where(left8, pltpu.roll(e, 64, 1), o)

    for q in range(3):
        span = recv2.at[q, pl.ds(0, PEERS - 1)]
        pltpu.make_async_copy(span, span, rsem2.at[q]).wait()
        pltpu.make_async_copy(recv2.at[q, 0], recv2.at[q, 0], lsem2.at[q]).wait()
        up, down = halos(q)
        up.start()
        down.start()

        def own(k, carry):
            unpack(lambda i, at, n: recv2[q, i, at : at + n, :].astype(F32), k * 4, k + 1, k)
            return carry

        lax.fori_loop(0, 16, own, 0)
        up.wait_recv()
        down.wait_recv()
        unpack(lambda i, at, n: low[q, i, at : at + n, :].astype(F32), 0, 0, None)
        unpack(lambda i, at, n: high[q, i, at : at + n, :].astype(F32), 0, 17, None)

        def derive(k, carry):
            index = row * 16 + k
            r = 0.5 + (jnp.full((16, 128), index.astype(F32), F32) + 0.5) * (1.0 / total)
            inv = 1.0 / r
            bottom, top = index == 0, index == total - 1
            hi = jnp.where(top, 0.0, jnp.where(bottom, 1.0, 0.5)) * inv
            mid = jnp.where(bottom, -1.0, jnp.where(top, 1.0, 0.0)) * inv
            lo = jnp.where(bottom, 0.0, jnp.where(top, -1.0, -0.5)) * inv
            for pair in range(2):

                def diff(at):
                    here = lambda n: full[pair, aligned(at + (k + n) * 16, 16), :]
                    return hi * here(2) + mid * here(1) + lo * here(0)

                lhs[pair, aligned(256 + k * 16, 16), :] = -diff(288)
                lhs[pair, aligned(512 + k * 16, 16), :] = diff(0)
            return carry

        lax.fori_loop(0, 16, derive, 0)

        for s in range(8):
            x = jnp.concatenate(
                [lhs[0, pl.ds(s, 96, stride=8), :], lhs[1, pl.ds(s, 96, stride=8), :]], axis=1
            ).astype(BF16)
            table = jnp.concatenate(
                [leg[s, :, q * 128 : q * 128 + 128], leg[s, :, q * 128 + 384 : q * 128 + 512]],
                axis=1,
            )
            y = lax.dot_general(x, table, (((1,), (1,)), ((), ())), preferred_element_type=F32)
            if q == 2:
                degree = lax.broadcasted_iota(jnp.int32, y.shape, 1)
                y = jnp.where(degree >= assign_ref[me * 8 + s], done[s] + y, 0.0)
                for t in range(4):
                    coef[t, pl.ds(s, 96, stride=8), :] = y[:, t * 128 : t * 128 + 128]
            else:
                done[s] = y if q == 0 else done[s] + y

    for t in range(4):
        out_ref[:, t * 128 : t * 128 + 128] = coef[t, 0:768, :]

    for q in range(3):
        span = send1.at[q, pl.ds(0, PEERS - 1)]
        pltpu.make_async_copy(span, span, ssem1.at[q]).wait()
        span = send2.at[q, pl.ds(0, PEERS - 1)]
        pltpu.make_async_copy(span, span, ssem2.at[q]).wait()
        up, down = halos(q)
        up.wait_send()
        down.wait_send()


def shards(fields, legendre, quad, assign):
    order = jnp.broadcast_to(assign.reshape(64, 1, 8), (64, 2, 8)).reshape(1, 1024)
    vmem = pl.BlockSpec(memory_space=pltpu.VMEM)
    hbm = pl.BlockSpec(memory_space=pl.ANY)
    dma = pltpu.SemaphoreType.DMA
    result = pl.pallas_call(
        kernel,
        in_specs=[pl.BlockSpec(memory_space=pltpu.SMEM), vmem, vmem, hbm, hbm],
        out_specs=vmem,
        out_shape=jax.ShapeDtypeStruct((768, 512), F32),
        scratch_shapes=[
            pltpu.VMEM((1536, 512), BF16),
            pltpu.VMEM((4, 1536, 128), F32),
            pltpu.VMEM((8, 192, 512), BF16),
            pltpu.VMEM((8, 512, 768), BF16),
            pltpu.VMEM((2, 1536, 128), F32),
            pltpu.VMEM((3, PEERS, 16, 384), BF16),
            pltpu.VMEM((3, PEERS, 16, 384), BF16),
            pltpu.VMEM((NLON, 1024), BF16),
            pltpu.VMEM((1024, NLON), BF16),
            pltpu.VMEM((128, 1024), F32),
            pltpu.VMEM((128, 1024), F32),
            pltpu.VMEM((16, 1024), F32),
            pltpu.VMEM((16, 1024), F32),
            pltpu.VMEM((NLON, 256), BF16),
            pltpu.VMEM((3, PEERS, 24, 128), BF16),
            pltpu.VMEM((3, PEERS, 24, 128), BF16),
            pltpu.VMEM((3, 4, 24, 128), BF16),
            pltpu.VMEM((3, 4, 24, 128), BF16),
            pltpu.VMEM((2, 576, 128), F32),
            pltpu.VMEM((2, 768, 128), F32),
            pltpu.VMEM((8, 96, 512), F32),
            dma((9,)),
            dma((3,)),
            dma((3,)),
            dma((3,)),
            dma((3,)),
            dma((3,)),
            dma((3,)),
            dma((6,)),
            dma((6,)),
        ],
        compiler_params=pltpu.CompilerParams(collective_id=0, has_side_effects=True),
        name="induction",
    )(assign, order, quad.reshape(6, 128), fields.reshape(1536, 512), legendre)
    return result.reshape(3, 16, 2, 8, 512)


def solution(mesh):
    return jax.shard_map(
        shards,
        mesh=mesh,
        in_specs=(P(None, "row", None, "ma", None), P("ma", None, None), P(), P()),
        out_specs=P(None, "row", None, "ma", None),
        check_vma=False,
    )
```

```python
import math

import jax
import jax.numpy as jnp
import numpy as np
from jax import lax
from jax.experimental import pallas as pl
from jax.experimental.pallas import tpu as pltpu
from jax.sharding import PartitionSpec as P

NLON = 1536
PEERS = 64
F32 = jnp.float32
BF16 = jnp.bfloat16
MESH = pl.DeviceIdType.MESH


def fit(function, terms):
    z = 0.125 - 0.1251 * np.cos(np.pi * (np.arange(400) + 0.5) / 400)
    z = np.clip(z, 1e-12, None)
    values = function(np.sqrt(z))
    basis = np.polynomial.Chebyshev.fit(z, values, terms - 1, domain=[0.0, 0.25])
    power = basis.convert(kind=np.polynomial.Polynomial)
    return [float(c) for c in power.coef]


COS = fit(lambda t: np.cos(2 * np.pi * t), 9)
SIN = fit(lambda t: np.sin(2 * np.pi * t) / t, 9)


def horner(coefs, z):
    total = jnp.full(z.shape, coefs[-1], F32)
    for c in coefs[-2::-1]:
        total = total * z + c
    return total


def cos_sin(product):
    turns = jnp.floor(product * (1.0 / NLON) + 0.5)
    t = (product - turns * NLON) * (1.0 / NLON)
    z = t * t
    return horner(COS, z), t * horner(SIN, z)


def aligned(value, size):
    return pl.ds(pl.multiple_of(value, size), size)


def kernel(
    small_ref, fields_hbm, leg_hbm, out_hbm,
    fbuf, coef, xs, leg, spat, send1, recv1, synth, analysis, cb, sb, ca, sa,
    emf, send2, recv2, send3, recv3, low, high, full, lhs, done, orders, quads,
    in_sem, ssem1, rsem1, lsem1, ssem2, rsem2, ssem3, rsem3, hsend, hrecv,
):
    me = lax.axis_index("ma")
    row = lax.axis_index("row")
    rows = lax.axis_size("row")
    above = lax.rem(row + 1, rows)
    below = lax.rem(row + rows - 1, rows)
    total = 16 * rows

    fetch = pltpu.make_async_copy(fields_hbm, fbuf, in_sem.at[8])
    fetch.start()
    fetches = [pltpu.make_async_copy(leg_hbm.at[s], leg.at[s], in_sem.at[s]) for s in range(8)]
    for f in fetches:
        f.start()

    barrier = pltpu.get_barrier_semaphore()

    def greet(i, carry):
        pl.semaphore_signal(
            barrier, inc=1, device_id={"ma": lax.rem(me + i, PEERS)}, device_id_type=MESH
        )
        return carry

    lax.fori_loop(1, PEERS, greet, 0)
    for other in (above, below):
        pl.semaphore_signal(barrier, inc=1, device_id={"row": other}, device_id_type=MESH)

    left = lax.broadcasted_iota(jnp.int32, (16, 128), 1) < 64

    fetch.wait()
    for t in range(4):
        coef[t] = fbuf[:, t * 128 : t * 128 + 128].astype(F32)

    def mask(s, carry):
        order = small_ref[me * 8 + s]
        for t in range(4):
            x = coef[t, pl.ds(s, 192, stride=8), :]
            degree = (lax.broadcasted_iota(jnp.int32, x.shape, 1) + t * 128).astype(F32)
            xs[s, :, t * 128 : t * 128 + 128] = jnp.where(degree >= order, x, 0.0).astype(BF16)
        return carry

    lax.fori_loop(0, 8, mask, 0)

    def level_group(i):
        half = (i + 1) // 2
        odd = lax.rem(i, 2)
        return lax.rem(me // 4 + odd * half + (1 - odd) * (16 - half), 16)

    def issue1(q, i):
        k = level_group(i)
        for jq in range(4):
            dest = k * 4 + jq

            @pl.when(dest != me)
            def _():
                pltpu.make_async_remote_copy(
                    src_ref=send1.at[q, dest],
                    dst_ref=recv1.at[q, me],
                    send_sem=ssem1.at[q],
                    recv_sem=rsem1.at[q],
                    device_id={"ma": dest},
                    device_id_type=MESH,
                ).start()

            @pl.when(dest == me)
            def _():
                pltpu.make_async_copy(send1.at[q, dest], recv1.at[q, me], lsem1.at[q]).start()

    for q in range(3):
        for s in range(8):
            if q == 0:
                fetches[s].wait()
            table = jnp.concatenate(
                [leg[s, :, q * 128 : q * 128 + 128], leg[s, :, q * 128 + 384 : q * 128 + 512]],
                axis=1,
            )
            y = jnp.dot(xs[s], table, preferred_element_type=F32)
            spat[0, pl.ds(s, 192, stride=8), :] = y[:, :128]
            spat[1, pl.ds(s, 192, stride=8), :] = y[:, 128:]

        def group(i, carry):
            k = level_group(i)
            for jq in range(4):
                for p in range(3):
                    u = spat[jq // 2, aligned(p * 256 + k * 16, 16), :]
                    b = spat[jq // 2, aligned(p * 256 + 768 + k * 16, 16), :]
                    if jq % 2:
                        v = jnp.where(left, pltpu.roll(u, 64, 1), b)
                    else:
                        v = jnp.where(left, u, pltpu.roll(b, 64, 1))
                    send1[q, k * 4 + jq, :, p * 128 : p * 128 + 128] = v.astype(BF16)

            if q > 0:

                @pl.when(i > 0)
                def _():
                    issue1(q, i - 1)

            return carry

        lax.fori_loop(0, 16, group, 0)
        if q == 0:
            pl.semaphore_wait(barrier, PEERS + 1)

            def send(i, carry):
                issue1(0, i)
                return carry

            lax.fori_loop(0, 15, send, 0)
        issue1(q, 15)

    lane1 = lax.broadcasted_iota(jnp.int32, (1, 128), 1)
    slot = (lane1 // 16) * 8 + lax.rem(lane1, 8)

    def spread(i, carry):
        held = jnp.zeros((1, 128), F32)
        for n in range(64):
            held = jnp.where(slot == n, small_ref[i * 64 + n], held)
        orders[0:1, aligned(i * 128, 128)] = held
        return carry

    lax.fori_loop(0, 8, spread, 0)
    jq = lax.rem(me, 4)
    for q in range(3):
        first = ((jq // 2) * 3 + q) * 128 + lax.rem(jq, 2) * 64
        held = jnp.zeros((1, 128), F32)
        for n in range(64):
            held = jnp.where(lax.rem(lane1, 64) == n, small_ref[PEERS * 8 + first + n], held)
        quads[q : q + 1, :] = held
    m = orders[0:1, :]
    lane = lax.broadcasted_iota(jnp.int32, (16, 1024), 1)
    second = lax.rem(lane // 8, 2) == 1
    n1 = lax.broadcasted_iota(jnp.int32, (16, 1024), 0).astype(F32) * 128.0
    c, s_ = cos_sin(n1 * m)
    ca[...] = jnp.where(second, -s_, c)
    sa[...] = jnp.where(second, c, s_)

    def fine(i, carry):
        n0 = (lax.broadcasted_iota(jnp.int32, (16, 1024), 0) + i * 16).astype(F32)
        c, s_ = cos_sin(n0 * m)
        cb[aligned(i * 16, 16), :] = c
        sb[aligned(i * 16, 16), :] = s_
        return carry

    lax.fori_loop(0, 8, fine, 0)
    factor = jnp.where(m > 0.0, 2.0, 1.0) * (1.0 / math.sqrt(PEERS * 8))
    for n in range(NLON // 128):
        cn = ca[n : n + 1, :] * factor
        sn = sa[n : n + 1, :] * factor

        def fill(i, carry):
            at = aligned(i * 16, 16)
            synth[aligned(n * 128 + i * 16, 16), :] = (cn * cb[at, :] - sn * sb[at, :]).astype(BF16)
            return carry

        lax.fori_loop(0, 8, fill, 0)

    def across(i, carry):
        at = aligned(i * 128, 128)
        cbt, sbt = cb[:, at].T, sb[:, at].T
        cat, sat = ca[:, at].T, sa[:, at].T
        scale = 1.0 / math.sqrt(NLON)
        cat, sat = cat * scale, sat * scale
        for n in range(NLON // 128):
            v = cat[:, n : n + 1] * cbt - sat[:, n : n + 1] * sbt
            analysis[at, n * 128 : n * 128 + 128] = v.astype(BF16)
        return carry

    lax.fori_loop(0, 8, across, 0)

    level = row * 16 + me // 4
    radius = 0.5 + (level.astype(F32) + 0.5) * (1.0 / total)
    left_tall = lax.broadcasted_iota(jnp.int32, (256, 128), 1) < 64

    def issue2(q, i, source, target, ssem, rsem):
        tile = lax.rem(me // 16 + i, 4)

        def one(j, carry):
            dest = tile * 16 + lax.rem(me + j, 16)

            @pl.when(dest != me)
            def _():
                pltpu.make_async_remote_copy(
                    src_ref=source.at[q, dest],
                    dst_ref=target.at[q, me],
                    send_sem=ssem.at[q],
                    recv_sem=rsem,
                    device_id={"ma": dest},
                    device_id_type=MESH,
                ).start()

            @pl.when(dest == me)
            def _():
                pltpu.make_async_copy(source.at[q, dest], target.at[q, me], rsem).start()

            return carry

        lax.fori_loop(0, 16, one, 0)

    def issue_parts(q, i):
        issue2(q, i, send2, recv2, ssem2, rsem2.at[q, me // 4])

    def issue_radial(q, i):
        issue2(q, i, send3, recv3, ssem3, rsem3.at[q])

    for q in range(3):
        span = recv1.at[q, pl.ds(0, PEERS - 1)]
        pltpu.make_async_copy(span, span, rsem1.at[q]).wait()
        pltpu.make_async_copy(recv1.at[q, 0], recv1.at[q, 0], lsem1.at[q]).wait()
        weight = quads[q : q + 1, :]

        def synthesise(i, carry):
            at = aligned(i * 256, 256)
            got = recv1[q].reshape(1024, 384)
            g = jnp.dot(synth[at, :], got, preferred_element_type=F32)
            c = [g[:, p * 128 : p * 128 + 128] for p in range(3)]
            r = [pltpu.roll(v, 64, 1) for v in c]
            d = []
            for a, b in ((1, 2), (2, 0), (0, 1)):
                t = c[a] * r[b]
                d.append(t - pltpu.roll(t, 64, 1))
            emf[at, 0:128] = (jnp.where(left_tall, d[1], -d[2]) * radius).astype(BF16)
            emf[at, 128:256] = d[0].astype(BF16)
            return carry

        lax.fori_loop(0, NLON // 256, synthesise, 0)

        def analyse(i, carry):
            tile = lax.rem(me // 16 + i, 4)
            w = jnp.dot(analysis[aligned(tile * 256, 256), :], emf[...], preferred_element_type=F32)
            dests = aligned(tile * 16, 16)
            send2[q, dests] = (w[:, :128] * weight).reshape(16, 16, 128).astype(BF16)
            last = (w[:, 128:] * weight).reshape(16, 16, 128)
            lane3 = lax.broadcasted_iota(jnp.int32, (16, 8, 128), 2)
            pair = jnp.where(lane3 < 64, last[:, :8], -last[:, 8:])
            send3[q, dests] = pair.astype(BF16)

            @pl.when(i > 0)
            def _():
                issue_parts(q, i - 1)

            return carry

        lax.fori_loop(0, 4, analyse, 0)
        issue_parts(q, 3)
        for i in range(4):
            issue_radial(q, i)

    left8 = lax.broadcasted_iota(jnp.int32, (8, 128), 1) < 64

    def halos(q):
        up = pltpu.make_async_remote_copy(
            src_ref=recv2.at[q, pl.ds(60, 4)],
            dst_ref=low.at[q],
            send_sem=hsend.at[2 * q],
            recv_sem=hrecv.at[2 * q],
            device_id={"row": above},
            device_id_type=MESH,
        )
        down = pltpu.make_async_remote_copy(
            src_ref=recv2.at[q, pl.ds(0, 4)],
            dst_ref=high.at[q],
            send_sem=hsend.at[2 * q + 1],
            recv_sem=hrecv.at[2 * q + 1],
            device_id={"row": below},
            device_id_type=MESH,
        )
        return up, down

    def unpack(block, first, level):
        for pair in range(2):
            e, o = block(first + pair * 2), block(first + pair * 2 + 1)
            full[pair, aligned(level * 16, 16), :] = jnp.where(left, e, pltpu.roll(o, 64, 1))
            full[pair, aligned(288 + level * 16, 16), :] = jnp.where(left, pltpu.roll(e, 64, 1), o)

    puts = [
        pltpu.make_async_copy(
            coef.at[t, pl.ds(0, 768)], out_hbm.at[:, pl.ds(t * 128, 128)], in_sem.at[t]
        )
        for t in range(4)
    ]

    for q in range(3):
        up, down = halos(q)

        def own(n, carry):
            k = lax.rem(me // 16 + 4 - n // 4, 4) * 4 + lax.rem(n, 4)
            span = recv2.at[q, pl.ds(k * 4, 4)]
            pltpu.make_async_copy(span, span, rsem2.at[q, k]).wait()

            @pl.when(k == 15)
            def _():
                up.start()

            @pl.when(k == 0)
            def _():
                down.start()

            unpack(lambda i: recv2[q, i].astype(F32), k * 4, k + 1)
            return carry

        lax.fori_loop(0, 16, own, 0)

        def derive(k, carry):
            index = row * 16 + k
            r = 0.5 + (jnp.full((16, 128), index.astype(F32), F32) + 0.5) * (1.0 / total)
            inv = 1.0 / r
            bottom, top = index == 0, index == total - 1
            hi = jnp.where(top, 0.0, jnp.where(bottom, 1.0, 0.5)) * inv
            mid = jnp.where(bottom, -1.0, jnp.where(top, 1.0, 0.0)) * inv
            lo = jnp.where(bottom, 0.0, jnp.where(top, -1.0, -0.5)) * inv
            for pair in range(2):

                def diff(at):
                    here = lambda n: full[pair, aligned(at + (k + n) * 16, 16), :]
                    return hi * here(2) + mid * here(1) + lo * here(0)

                lhs[pair, aligned(256 + k * 16, 16), :] = -diff(288)
                lhs[pair, aligned(512 + k * 16, 16), :] = diff(0)
            return carry

        lax.fori_loop(1, 15, derive, 0)
        up.wait_recv()
        down.wait_recv()
        unpack(lambda i: low[q, i].astype(F32), 0, 0)
        unpack(lambda i: high[q, i].astype(F32), 0, 17)
        derive(0, 0)
        derive(15, 0)

        pltpu.make_async_copy(recv3.at[q], recv3.at[q], rsem3.at[q]).wait()

        def radial(k, carry):
            for pair in range(2):
                e = recv3[q, k * 4 + pair * 2].astype(F32)
                o = recv3[q, k * 4 + pair * 2 + 1].astype(F32)
                lhs[pair, aligned(k * 16, 8), :] = jnp.where(left8, e, pltpu.roll(o, 64, 1))
                lhs[pair, aligned(k * 16 + 8, 8), :] = jnp.where(left8, pltpu.roll(e, 64, 1), o)
            return carry

        lax.fori_loop(0, 16, radial, 0)

        for half in range(2):
            lines = slice(half * 256, half * 256 + 256)
            for s in range(8):
                x = jnp.concatenate(
                    [lhs[0, pl.ds(s, 96, stride=8), :], lhs[1, pl.ds(s, 96, stride=8), :]], axis=1
                ).astype(BF16)
                table = jnp.concatenate(
                    [
                        leg[s, lines, q * 128 : q * 128 + 128],
                        leg[s, lines, q * 128 + 384 : q * 128 + 512],
                    ],
                    axis=1,
                )
                y = lax.dot_general(x, table, (((1,), (1,)), ((), ())), preferred_element_type=F32)
                if q > 0:
                    y = done[s, :, lines] + y
                if q < 2:
                    done[s, :, lines] = y
                else:
                    degree = lax.broadcasted_iota(jnp.int32, y.shape, 1) + half * 256
                    y = jnp.where(degree.astype(F32) >= small_ref[me * 8 + s], y, 0.0)
                    for t in range(2):
                        coef[half * 2 + t, pl.ds(s, 96, stride=8), :] = y[:, t * 128 : t * 128 + 128]
            if q == 2:
                for t in range(half * 2, half * 2 + 2):
                    puts[t].start()

    for q in range(3):
        span = send1.at[q, pl.ds(0, PEERS - 1)]
        pltpu.make_async_copy(span, span, ssem1.at[q]).wait()
        span = send2.at[q, pl.ds(0, PEERS - 1)]
        pltpu.make_async_copy(span, span, ssem2.at[q]).wait()
        span = send3.at[q, pl.ds(0, PEERS - 1)]
        pltpu.make_async_copy(span, span, ssem3.at[q]).wait()
        up, down = halos(q)
        up.wait_send()
        down.wait_send()
    for put in puts:
        put.wait()


def shards(fields, legendre, quad, assign):
    small = lax.pad(assign, jnp.int32(0), [(0, quad.shape[0], 0)]).astype(F32) + lax.pad(
        quad, F32(0), [(assign.shape[0], 0, 0)]
    )
    smem = pl.BlockSpec(memory_space=pltpu.SMEM)
    hbm = pl.BlockSpec(memory_space=pltpu.HBM)
    dma = pltpu.SemaphoreType.DMA
    result = pl.pallas_call(
        kernel,
        in_specs=[smem, hbm, hbm],
        out_specs=pl.BlockSpec(memory_space=pl.ANY),
        out_shape=jax.ShapeDtypeStruct((768, 512), F32),
        scratch_shapes=[
            pltpu.VMEM((1536, 512), BF16),
            pltpu.VMEM((4, 1536, 128), F32),
            pltpu.VMEM((8, 192, 512), BF16),
            pltpu.VMEM((8, 512, 768), BF16),
            pltpu.VMEM((2, 1536, 128), F32),
            pltpu.VMEM((3, PEERS, 16, 384), BF16),
            pltpu.VMEM((3, PEERS, 16, 384), BF16),
            pltpu.VMEM((NLON, 1024), BF16),
            pltpu.VMEM((1024, NLON), BF16),
            pltpu.VMEM((128, 1024), F32),
            pltpu.VMEM((128, 1024), F32),
            pltpu.VMEM((16, 1024), F32),
            pltpu.VMEM((16, 1024), F32),
            pltpu.VMEM((NLON, 256), BF16),
            pltpu.VMEM((3, PEERS, 16, 128), BF16),
            pltpu.VMEM((3, PEERS, 16, 128), BF16),
            pltpu.VMEM((3, PEERS, 8, 128), BF16),
            pltpu.VMEM((3, PEERS, 8, 128), BF16),
            pltpu.VMEM((3, 4, 16, 128), BF16),
            pltpu.VMEM((3, 4, 16, 128), BF16),
            pltpu.VMEM((2, 576, 128), F32),
            pltpu.VMEM((2, 768, 128), F32),
            pltpu.VMEM((8, 96, 512), F32),
            pltpu.VMEM((8, 1024), F32),
            pltpu.VMEM((8, 128), F32),
            dma((9,)),
            dma((3,)),
            dma((3,)),
            dma((3,)),
            dma((3,)),
            dma((3, 16)),
            dma((3,)),
            dma((3,)),
            dma((6,)),
            dma((6,)),
        ],
        compiler_params=pltpu.CompilerParams(
            collective_id=0, has_side_effects=True, vmem_limit_bytes=54_000_000
        ),
        name="induction",
    )(small, fields.reshape(1536, 512), legendre)
    return result.reshape(3, 16, 2, 8, 512)


def solution(mesh):
    return jax.shard_map(
        shards,
        mesh=mesh,
        in_specs=(P(None, "row", None, "ma", None), P("ma", None, None), P(), P()),
        out_specs=P(None, "row", None, "ma", None),
        check_vma=False,
    )
```

```python
import math

import jax
import jax.numpy as jnp
import numpy as np
from jax import lax
from jax.experimental import pallas as pl
from jax.experimental.pallas import tpu as pltpu
from jax.sharding import PartitionSpec as P

NLON = 1536
PEERS = 64
F32 = jnp.float32
BF16 = jnp.bfloat16
MESH = pl.DeviceIdType.MESH


def fit(function, terms):
    z = 0.125 - 0.1251 * np.cos(np.pi * (np.arange(400) + 0.5) / 400)
    z = np.clip(z, 1e-12, None)
    values = function(np.sqrt(z))
    basis = np.polynomial.Chebyshev.fit(z, values, terms - 1, domain=[0.0, 0.25])
    power = basis.convert(kind=np.polynomial.Polynomial)
    return [float(c) for c in power.coef]


COS = fit(lambda t: np.cos(2 * np.pi * t), 9)
SIN = fit(lambda t: np.sin(2 * np.pi * t) / t, 9)


def horner(coefs, z):
    total = jnp.full(z.shape, coefs[-1], F32)
    for c in coefs[-2::-1]:
        total = total * z + c
    return total


def cos_sin(product):
    turns = jnp.floor(product * (1.0 / NLON) + 0.5)
    t = (product - turns * NLON) * (1.0 / NLON)
    z = t * t
    return horner(COS, z), t * horner(SIN, z)


def aligned(value, size):
    return pl.ds(pl.multiple_of(value, size), size)


def kernel(
    small_ref, fields_hbm, leg_hbm, out_hbm,
    fbuf, coef, xs, leg, spat, send1, recv1, synth, analysis, cb, sb, ca, sa,
    emf, send2, recv2, low, high, full, lhs, done, orders, quads,
    in_sem, ssem1, rsem1, lsem1, ssem2, rsem2, ssem3, rsem3, hsend, hrecv,
):
    me = lax.axis_index("ma")
    row = lax.axis_index("row")
    rows = lax.axis_size("row")
    above = lax.rem(row + 1, rows)
    below = lax.rem(row + rows - 1, rows)
    total = 16 * rows

    fetch = pltpu.make_async_copy(fields_hbm, fbuf, in_sem.at[8])
    fetch.start()
    fetches = [pltpu.make_async_copy(leg_hbm.at[s], leg.at[s], in_sem.at[s]) for s in range(8)]
    for f in fetches:
        f.start()

    barrier = pltpu.get_barrier_semaphore()

    def greet(i, carry):
        pl.semaphore_signal(
            barrier, inc=1, device_id={"ma": lax.rem(me + i, PEERS)}, device_id_type=MESH
        )
        return carry

    lax.fori_loop(1, PEERS, greet, 0)
    for other in (above, below):
        pl.semaphore_signal(barrier, inc=1, device_id={"row": other}, device_id_type=MESH)

    left = lax.broadcasted_iota(jnp.int32, (16, 128), 1) < 64

    fetch.wait()
    for t in range(4):
        coef[t] = fbuf[:, t * 128 : t * 128 + 128].astype(F32)

    def mask(s, carry):
        order = small_ref[me * 8 + s]
        for t in range(4):
            x = coef[t, pl.ds(s, 192, stride=8), :]
            degree = (lax.broadcasted_iota(jnp.int32, x.shape, 1) + t * 128).astype(F32)
            xs[s, :, t * 128 : t * 128 + 128] = jnp.where(degree >= order, x, 0.0).astype(BF16)
        return carry

    lax.fori_loop(0, 8, mask, 0)

    def level_group(i):
        half = (i + 1) // 2
        odd = lax.rem(i, 2)
        return lax.rem(me // 4 + odd * half + (1 - odd) * (16 - half), 16)

    def issue1(q, i):
        k = level_group(i)
        for jq in range(4):
            dest = k * 4 + jq

            @pl.when(dest != me)
            def _():
                pltpu.make_async_remote_copy(
                    src_ref=send1.at[q, dest],
                    dst_ref=recv1.at[q, me],
                    send_sem=ssem1.at[q],
                    recv_sem=rsem1.at[q],
                    device_id={"ma": dest},
                    device_id_type=MESH,
                ).start()

            @pl.when(dest == me)
            def _():
                pltpu.make_async_copy(send1.at[q, dest], recv1.at[q, me], lsem1.at[q]).start()

    for q in range(3):
        for s in range(8):
            if q == 0:
                fetches[s].wait()
            table = jnp.concatenate(
                [leg[s, :, q * 128 : q * 128 + 128], leg[s, :, q * 128 + 384 : q * 128 + 512]],
                axis=1,
            )
            y = jnp.dot(xs[s], table, preferred_element_type=F32)
            spat[0, pl.ds(s, 192, stride=8), :] = y[:, :128]
            spat[1, pl.ds(s, 192, stride=8), :] = y[:, 128:]

        def group(i, carry):
            k = level_group(i)
            for jq in range(4):
                for p in range(3):
                    u = spat[jq // 2, aligned(p * 256 + k * 16, 16), :]
                    b = spat[jq // 2, aligned(p * 256 + 768 + k * 16, 16), :]
                    if jq % 2:
                        v = jnp.where(left, pltpu.roll(u, 64, 1), b)
                    else:
                        v = jnp.where(left, u, pltpu.roll(b, 64, 1))
                    send1[q, k * 4 + jq, :, p * 128 : p * 128 + 128] = v.astype(BF16)

            return carry

        def group_and_send(i, carry):
            group(i, carry)
            issue1(q, i - lag)
            return carry

        def send(i, carry):
            issue1(q, i)
            return carry

        lag = 3 if q == 0 else 1
        lax.fori_loop(0, lag, group, 0)
        if q == 0:
            pl.semaphore_wait(barrier, PEERS + 1)
        lax.fori_loop(lag, 16, group_and_send, 0)
        lax.fori_loop(16 - lag, 16, send, 0)

    lane1 = lax.broadcasted_iota(jnp.int32, (1, 128), 1)
    slot = (lane1 // 16) * 8 + lax.rem(lane1, 8)

    def spread(i, carry):
        held = jnp.zeros((1, 128), F32)
        for n in range(64):
            held = jnp.where(slot == n, small_ref[i * 64 + n], held)
        orders[0:1, aligned(i * 128, 128)] = held
        return carry

    lax.fori_loop(0, 8, spread, 0)
    jq = lax.rem(me, 4)
    for q in range(3):
        first = ((jq // 2) * 3 + q) * 128 + lax.rem(jq, 2) * 64
        held = jnp.zeros((1, 128), F32)
        for n in range(64):
            held = jnp.where(lax.rem(lane1, 64) == n, small_ref[PEERS * 8 + first + n], held)
        quads[q : q + 1, :] = held
    m = orders[0:1, :]
    lane = lax.broadcasted_iota(jnp.int32, (16, 1024), 1)
    second = lax.rem(lane // 8, 2) == 1
    n1 = lax.broadcasted_iota(jnp.int32, (16, 1024), 0).astype(F32) * 128.0
    c, s_ = cos_sin(n1 * m)
    ca[...] = jnp.where(second, -s_, c)
    sa[...] = jnp.where(second, c, s_)

    def fine(i, carry):
        n0 = (lax.broadcasted_iota(jnp.int32, (16, 1024), 0) + i * 16).astype(F32)
        c, s_ = cos_sin(n0 * m)
        cb[aligned(i * 16, 16), :] = c
        sb[aligned(i * 16, 16), :] = s_
        return carry

    lax.fori_loop(0, 8, fine, 0)
    factor = jnp.where(m > 0.0, 2.0, 1.0) * (1.0 / math.sqrt(PEERS * 8))
    for n in range(NLON // 128):
        cn = ca[n : n + 1, :] * factor
        sn = sa[n : n + 1, :] * factor

        def fill(i, carry):
            at = aligned(i * 16, 16)
            synth[aligned(n * 128 + i * 16, 16), :] = (cn * cb[at, :] - sn * sb[at, :]).astype(BF16)
            return carry

        lax.fori_loop(0, 8, fill, 0)

    def across(i, carry):
        at = aligned(i * 128, 128)
        cbt, sbt = cb[:, at].T, sb[:, at].T
        cat, sat = ca[:, at].T, sa[:, at].T
        scale = 1.0 / math.sqrt(NLON)
        cat, sat = cat * scale, sat * scale
        for n in range(NLON // 128):
            v = cat[:, n : n + 1] * cbt - sat[:, n : n + 1] * sbt
            analysis[at, n * 128 : n * 128 + 128] = v.astype(BF16)
        return carry

    lax.fori_loop(0, 8, across, 0)

    level = row * 16 + me // 4
    radius = 0.5 + (level.astype(F32) + 0.5) * (1.0 / total)
    left_tall = lax.broadcasted_iota(jnp.int32, (256, 128), 1) < 64

    def part(ref, q, index, which):
        if q < 2:
            return ref.at[q, index]
        return ref.at[q, index, pl.ds(0, 16) if which == 0 else pl.ds(16, 8)]

    def issue2(q, i, which):
        tile = lax.rem(me // 16 + i, 4)
        ssem = ssem2.at[q] if which == 0 else ssem3.at[0]
        rsem = rsem2.at[q, me // 4] if which == 0 else rsem3.at[0]

        def one(j, carry):
            dest = tile * 16 + lax.rem(me + j, 16)
            source, target = part(send2, q, dest, which), part(recv2, q, me, which)

            @pl.when(dest != me)
            def _():
                pltpu.make_async_remote_copy(
                    src_ref=source,
                    dst_ref=target,
                    send_sem=ssem,
                    recv_sem=rsem,
                    device_id={"ma": dest},
                    device_id_type=MESH,
                ).start()

            @pl.when(dest == me)
            def _():
                pltpu.make_async_copy(source, target, rsem).start()

            return carry

        lax.fori_loop(0, 16, one, 0)

    for q in range(3):
        span = recv1.at[q, pl.ds(0, PEERS - 1)]
        pltpu.make_async_copy(span, span, rsem1.at[q]).wait()
        pltpu.make_async_copy(recv1.at[q, 0], recv1.at[q, 0], lsem1.at[q]).wait()
        weight = quads[q : q + 1, :]

        def synthesise(i, carry):
            at = aligned(i * 256, 256)
            got = recv1[q].reshape(1024, 384)
            g = jnp.dot(synth[at, :], got, preferred_element_type=F32)
            c = [g[:, p * 128 : p * 128 + 128] for p in range(3)]
            r = [pltpu.roll(v, 64, 1) for v in c]
            d = []
            for a, b in ((1, 2), (2, 0), (0, 1)):
                t = c[a] * r[b]
                d.append(t - pltpu.roll(t, 64, 1))
            emf[at, 0:128] = (jnp.where(left_tall, d[1], -d[2]) * radius).astype(BF16)
            emf[at, 128:256] = d[0].astype(BF16)
            return carry

        lax.fori_loop(0, NLON // 256, synthesise, 0)

        def analyse(i, carry):
            tile = lax.rem(me // 16 + i, 4)
            w = jnp.dot(analysis[aligned(tile * 256, 256), :], emf[...], preferred_element_type=F32)
            dests = aligned(tile * 16, 16)
            send2[q, dests, 0:16, :] = (w[:, :128] * weight).reshape(16, 16, 128).astype(BF16)
            last = (w[:, 128:] * weight).reshape(16, 16, 128)
            lane3 = lax.broadcasted_iota(jnp.int32, (16, 8, 128), 2)
            pair = jnp.where(lane3 < 64, last[:, :8], -last[:, 8:])
            send2[q, dests, 16:24, :] = pair.astype(BF16)

            @pl.when(i > 0)
            def _():
                issue2(q, i - 1, 0)

            return carry

        lax.fori_loop(0, 4, analyse, 0)
        issue2(q, 3, 0)
        if q == 2:
            for i in range(4):
                issue2(q, i, 1)

    left8 = lax.broadcasted_iota(jnp.int32, (8, 128), 1) < 64

    def halos(q):
        up = pltpu.make_async_remote_copy(
            src_ref=recv2.at[q, pl.ds(60, 4), pl.ds(0, 16)],
            dst_ref=low.at[q],
            send_sem=hsend.at[2 * q],
            recv_sem=hrecv.at[2 * q],
            device_id={"row": above},
            device_id_type=MESH,
        )
        down = pltpu.make_async_remote_copy(
            src_ref=recv2.at[q, pl.ds(0, 4), pl.ds(0, 16)],
            dst_ref=high.at[q],
            send_sem=hsend.at[2 * q + 1],
            recv_sem=hrecv.at[2 * q + 1],
            device_id={"row": below},
            device_id_type=MESH,
        )
        return up, down

    def unpack(block, first, level):
        for pair in range(2):
            e, o = block(first + pair * 2), block(first + pair * 2 + 1)
            full[pair, aligned(level * 16, 16), :] = jnp.where(left, e, pltpu.roll(o, 64, 1))
            full[pair, aligned(288 + level * 16, 16), :] = jnp.where(left, pltpu.roll(e, 64, 1), o)

    puts = [
        pltpu.make_async_copy(
            coef.at[t, pl.ds(0, 768)], out_hbm.at[:, pl.ds(t * 128, 128)], in_sem.at[t]
        )
        for t in range(4)
    ]

    for q in range(3):
        up, down = halos(q)

        def own(n, carry):
            k = lax.rem(me // 16 + 4 - n // 4, 4) * 4 + lax.rem(n, 4)
            span = part(recv2, q, pl.ds(k * 4, 4), 0)
            pltpu.make_async_copy(span, span, rsem2.at[q, k]).wait()

            @pl.when(k == 15)
            def _():
                up.start()

            @pl.when(k == 0)
            def _():
                down.start()

            unpack(lambda i: recv2[q, i, 0:16, :].astype(F32), k * 4, k + 1)
            return carry

        lax.fori_loop(0, 16, own, 0)

        def derive(k, carry):
            index = row * 16 + k
            r = 0.5 + (jnp.full((16, 128), index.astype(F32), F32) + 0.5) * (1.0 / total)
            inv = 1.0 / r
            bottom, top = index == 0, index == total - 1
            hi = jnp.where(top, 0.0, jnp.where(bottom, 1.0, 0.5)) * inv
            mid = jnp.where(bottom, -1.0, jnp.where(top, 1.0, 0.0)) * inv
            lo = jnp.where(bottom, 0.0, jnp.where(top, -1.0, -0.5)) * inv
            for pair in range(2):

                def diff(at):
                    here = lambda n: full[pair, aligned(at + (k + n) * 16, 16), :]
                    return hi * here(2) + mid * here(1) + lo * here(0)

                lhs[pair, aligned(256 + k * 16, 16), :] = -diff(288)
                lhs[pair, aligned(512 + k * 16, 16), :] = diff(0)
            return carry

        lax.fori_loop(1, 15, derive, 0)
        up.wait_recv()
        down.wait_recv()
        unpack(lambda i: low[q, i].astype(F32), 0, 0)
        unpack(lambda i: high[q, i].astype(F32), 0, 17)
        derive(0, 0)
        derive(15, 0)

        if q == 2:
            span = part(recv2, q, pl.ds(0, PEERS), 1)
            pltpu.make_async_copy(span, span, rsem3.at[0]).wait()

        def radial(k, carry):
            for pair in range(2):
                e = recv2[q, k * 4 + pair * 2, 16:24, :].astype(F32)
                o = recv2[q, k * 4 + pair * 2 + 1, 16:24, :].astype(F32)
                lhs[pair, aligned(k * 16, 8), :] = jnp.where(left8, e, pltpu.roll(o, 64, 1))
                lhs[pair, aligned(k * 16 + 8, 8), :] = jnp.where(left8, pltpu.roll(e, 64, 1), o)
            return carry

        lax.fori_loop(0, 16, radial, 0)

        for half in range(2):
            lines = slice(half * 256, half * 256 + 256)
            for s in range(8):
                x = jnp.concatenate(
                    [lhs[0, pl.ds(s, 96, stride=8), :], lhs[1, pl.ds(s, 96, stride=8), :]], axis=1
                ).astype(BF16)
                table = jnp.concatenate(
                    [
                        leg[s, lines, q * 128 : q * 128 + 128],
                        leg[s, lines, q * 128 + 384 : q * 128 + 512],
                    ],
                    axis=1,
                )
                y = lax.dot_general(x, table, (((1,), (1,)), ((), ())), preferred_element_type=F32)
                if q > 0:
                    y = done[s, :, lines] + y
                if q < 2:
                    done[s, :, lines] = y
                else:
                    degree = lax.broadcasted_iota(jnp.int32, y.shape, 1) + half * 256
                    y = jnp.where(degree.astype(F32) >= small_ref[me * 8 + s], y, 0.0)
                    for t in range(2):
                        coef[half * 2 + t, pl.ds(s, 96, stride=8), :] = y[:, t * 128 : t * 128 + 128]
            if q == 2:
                for t in range(half * 2, half * 2 + 2):
                    puts[t].start()

    for q in range(3):
        span = send1.at[q, pl.ds(0, PEERS - 1)]
        pltpu.make_async_copy(span, span, ssem1.at[q]).wait()
        span = part(send2, q, pl.ds(0, PEERS - 1), 0)
        pltpu.make_async_copy(span, span, ssem2.at[q]).wait()
        if q == 2:
            span = part(send2, q, pl.ds(0, PEERS - 1), 1)
            pltpu.make_async_copy(span, span, ssem3.at[0]).wait()
        up, down = halos(q)
        up.wait_send()
        down.wait_send()
    for put in puts:
        put.wait()


def shards(fields, legendre, quad, assign):
    small = lax.pad(assign, jnp.int32(0), [(0, quad.shape[0], 0)]).astype(F32) + lax.pad(
        quad, F32(0), [(assign.shape[0], 0, 0)]
    )
    smem = pl.BlockSpec(memory_space=pltpu.SMEM)
    hbm = pl.BlockSpec(memory_space=pltpu.HBM)
    dma = pltpu.SemaphoreType.DMA
    result = pl.pallas_call(
        kernel,
        in_specs=[smem, hbm, hbm],
        out_specs=pl.BlockSpec(memory_space=pl.ANY),
        out_shape=jax.ShapeDtypeStruct((768, 512), F32),
        scratch_shapes=[
            pltpu.VMEM((1536, 512), BF16),
            pltpu.VMEM((4, 1536, 128), F32),
            pltpu.VMEM((8, 192, 512), BF16),
            pltpu.VMEM((8, 512, 768), BF16),
            pltpu.VMEM((2, 1536, 128), F32),
            pltpu.VMEM((3, PEERS, 16, 384), BF16),
            pltpu.VMEM((3, PEERS, 16, 384), BF16),
            pltpu.VMEM((NLON, 1024), BF16),
            pltpu.VMEM((1024, NLON), BF16),
            pltpu.VMEM((128, 1024), F32),
            pltpu.VMEM((128, 1024), F32),
            pltpu.VMEM((16, 1024), F32),
            pltpu.VMEM((16, 1024), F32),
            pltpu.VMEM((NLON, 256), BF16),
            pltpu.VMEM((3, PEERS, 24, 128), BF16),
            pltpu.VMEM((3, PEERS, 24, 128), BF16),
            pltpu.VMEM((3, 4, 16, 128), BF16),
            pltpu.VMEM((3, 4, 16, 128), BF16),
            pltpu.VMEM((2, 576, 128), F32),
            pltpu.VMEM((2, 768, 128), F32),
            pltpu.VMEM((8, 96, 512), F32),
            pltpu.VMEM((8, 1024), F32),
            pltpu.VMEM((8, 128), F32),
            dma((9,)),
            dma((3,)),
            dma((3,)),
            dma((3,)),
            dma((3,)),
            dma((3, 16)),
            dma((1,)),
            dma((1,)),
            dma((6,)),
            dma((6,)),
        ],
        compiler_params=pltpu.CompilerParams(
            collective_id=0, has_side_effects=True, vmem_limit_bytes=54_000_000
        ),
        name="induction",
    )(small, fields.reshape(1536, 512), legendre)
    return result.reshape(3, 16, 2, 8, 512)


def solution(mesh):
    return jax.shard_map(
        shards,
        mesh=mesh,
        in_specs=(P(None, "row", None, "ma", None), P("ma", None, None), P(), P()),
        out_specs=P(None, "row", None, "ma", None),
        check_vma=False,
    )
```

```python
import math

import jax
import jax.numpy as jnp
import numpy as np
from jax import lax
from jax.experimental import pallas as pl
from jax.experimental.pallas import tpu as pltpu
from jax.sharding import PartitionSpec as P

NLON = 1536
PEERS = 64
F32 = jnp.float32
BF16 = jnp.bfloat16
MESH = pl.DeviceIdType.MESH


def fit(function, terms):
    z = 0.125 - 0.1251 * np.cos(np.pi * (np.arange(400) + 0.5) / 400)
    z = np.clip(z, 1e-12, None)
    values = function(np.sqrt(z))
    basis = np.polynomial.Chebyshev.fit(z, values, terms - 1, domain=[0.0, 0.25])
    power = basis.convert(kind=np.polynomial.Polynomial)
    return [float(c) for c in power.coef]


COS = fit(lambda t: np.cos(2 * np.pi * t), 9)
SIN = fit(lambda t: np.sin(2 * np.pi * t) / t, 9)


def horner(coefs, z):
    total = jnp.full(z.shape, coefs[-1], F32)
    for c in coefs[-2::-1]:
        total = total * z + c
    return total


def cos_sin(product):
    turns = jnp.floor(product * (1.0 / NLON) + 0.5)
    t = (product - turns * NLON) * (1.0 / NLON)
    z = t * t
    return horner(COS, z), t * horner(SIN, z)


def aligned(value, size):
    return pl.ds(pl.multiple_of(value, size), size)


def kernel(
    small_ref, fields_hbm, leg_hbm, out_hbm,
    fbuf, coef, xs, leg, spat, send1, recv1, synth, analysis, cb, sb, ca, sa,
    emf, send2, recv2, low, high, full, lhs, done, orders, quads,
    in_sem, ssem1, rsem1, lsem1, ssem2, rsem2, ssem3, rsem3, hsend, hrecv,
):
    me = lax.axis_index("ma")
    row = lax.axis_index("row")
    rows = lax.axis_size("row")
    above = lax.rem(row + 1, rows)
    below = lax.rem(row + rows - 1, rows)
    total = 16 * rows

    fetch = pltpu.make_async_copy(fields_hbm, fbuf, in_sem.at[8])
    fetch.start()
    fetches = []
    for t in (0, 3, 1, 4, 2, 5):
        lanes = pl.ds(t * 128, 128)
        fetches.append(
            pltpu.make_async_copy(leg_hbm.at[:, :, lanes], leg.at[:, :, lanes], in_sem.at[t])
        )
    for f in fetches:
        f.start()

    barrier = pltpu.get_barrier_semaphore()

    def greet(i, carry):
        pl.semaphore_signal(
            barrier, inc=1, device_id={"ma": lax.rem(me + i, PEERS)}, device_id_type=MESH
        )
        return carry

    lax.fori_loop(1, PEERS, greet, 0)
    for other in (above, below):
        pl.semaphore_signal(barrier, inc=1, device_id={"row": other}, device_id_type=MESH)

    left = lax.broadcasted_iota(jnp.int32, (16, 128), 1) < 64

    fetch.wait()
    for t in range(4):
        coef[t] = fbuf[:, t * 128 : t * 128 + 128].astype(F32)

    def mask(s, carry):
        order = small_ref[me * 8 + s]
        for t in range(4):
            x = coef[t, pl.ds(s, 192, stride=8), :]
            degree = (lax.broadcasted_iota(jnp.int32, x.shape, 1) + t * 128).astype(F32)
            xs[s, :, t * 128 : t * 128 + 128] = jnp.where(degree >= order, x, 0.0).astype(BF16)
        return carry

    lax.fori_loop(0, 8, mask, 0)

    def level_group(i):
        half = (i + 1) // 2
        odd = lax.rem(i, 2)
        return lax.rem(me // 4 + odd * half + (1 - odd) * (16 - half), 16)

    def issue1(q, i):
        k = level_group(i)
        for jq in range(4):
            dest = k * 4 + jq

            @pl.when(dest != me)
            def _():
                pltpu.make_async_remote_copy(
                    src_ref=send1.at[q, dest],
                    dst_ref=recv1.at[q, me],
                    send_sem=ssem1.at[q],
                    recv_sem=rsem1.at[q],
                    device_id={"ma": dest},
                    device_id_type=MESH,
                ).start()

            @pl.when(dest == me)
            def _():
                pltpu.make_async_copy(send1.at[q, dest], recv1.at[q, me], lsem1.at[q]).start()

    for q in range(3):
        fetches[2 * q].wait()
        fetches[2 * q + 1].wait()
        for s in range(8):
            table = jnp.concatenate(
                [leg[s, :, q * 128 : q * 128 + 128], leg[s, :, q * 128 + 384 : q * 128 + 512]],
                axis=1,
            )
            y = jnp.dot(xs[s], table, preferred_element_type=F32)
            spat[0, pl.ds(s, 192, stride=8), :] = y[:, :128]
            spat[1, pl.ds(s, 192, stride=8), :] = y[:, 128:]

        def group(i, carry):
            k = level_group(i)
            for jq in range(4):
                for p in range(3):
                    u = spat[jq // 2, aligned(p * 256 + k * 16, 16), :]
                    b = spat[jq // 2, aligned(p * 256 + 768 + k * 16, 16), :]
                    if jq % 2:
                        v = jnp.where(left, pltpu.roll(u, 64, 1), b)
                    else:
                        v = jnp.where(left, u, pltpu.roll(b, 64, 1))
                    send1[q, k * 4 + jq, :, p * 128 : p * 128 + 128] = v.astype(BF16)

            return carry

        def group_and_send(i, carry):
            group(i, carry)
            issue1(q, i - lag)
            return carry

        def send(i, carry):
            issue1(q, i)
            return carry

        lag = 3 if q == 0 else 1
        lax.fori_loop(0, lag, group, 0)
        if q == 0:
            pl.semaphore_wait(barrier, PEERS + 1)
        lax.fori_loop(lag, 16, group_and_send, 0)
        lax.fori_loop(16 - lag, 16, send, 0)

    lane1 = lax.broadcasted_iota(jnp.int32, (1, 128), 1)
    slot = (lane1 // 16) * 8 + lax.rem(lane1, 8)

    def spread(i, carry):
        held = jnp.zeros((1, 128), F32)
        for n in range(64):
            held = jnp.where(slot == n, small_ref[i * 64 + n], held)
        orders[0:1, aligned(i * 128, 128)] = held
        return carry

    lax.fori_loop(0, 8, spread, 0)
    jq = lax.rem(me, 4)
    for q in range(3):
        first = ((jq // 2) * 3 + q) * 128 + lax.rem(jq, 2) * 64
        held = jnp.zeros((1, 128), F32)
        for n in range(64):
            held = jnp.where(lax.rem(lane1, 64) == n, small_ref[PEERS * 8 + first + n], held)
        quads[q : q + 1, :] = held
    m = orders[0:1, :]
    lane = lax.broadcasted_iota(jnp.int32, (16, 1024), 1)
    second = lax.rem(lane // 8, 2) == 1
    n1 = lax.broadcasted_iota(jnp.int32, (16, 1024), 0).astype(F32) * 128.0
    c, s_ = cos_sin(n1 * m)
    ca[...] = jnp.where(second, -s_, c)
    sa[...] = jnp.where(second, c, s_)

    def fine(i, carry):
        n0 = (lax.broadcasted_iota(jnp.int32, (16, 1024), 0) + i * 16).astype(F32)
        c, s_ = cos_sin(n0 * m)
        cb[aligned(i * 16, 16), :] = c
        sb[aligned(i * 16, 16), :] = s_
        return carry

    lax.fori_loop(0, 8, fine, 0)
    factor = jnp.where(m > 0.0, 2.0, 1.0) * (1.0 / math.sqrt(PEERS * 8))
    for n in range(NLON // 128):
        cn = ca[n : n + 1, :] * factor
        sn = sa[n : n + 1, :] * factor

        def fill(i, carry):
            at = aligned(i * 16, 16)
            synth[aligned(n * 128 + i * 16, 16), :] = (cn * cb[at, :] - sn * sb[at, :]).astype(BF16)
            return carry

        lax.fori_loop(0, 8, fill, 0)

    def across(i, carry):
        at = aligned(i * 128, 128)
        cbt, sbt = cb[:, at].T, sb[:, at].T
        cat, sat = ca[:, at].T, sa[:, at].T
        scale = 1.0 / math.sqrt(NLON)
        cat, sat = cat * scale, sat * scale
        for n in range(NLON // 128):
            v = cat[:, n : n + 1] * cbt - sat[:, n : n + 1] * sbt
            analysis[at, n * 128 : n * 128 + 128] = v.astype(BF16)
        return carry

    lax.fori_loop(0, 8, across, 0)

    level = row * 16 + me // 4
    radius = 0.5 + (level.astype(F32) + 0.5) * (1.0 / total)
    left_tall = lax.broadcasted_iota(jnp.int32, (256, 128), 1) < 64

    def part(ref, q, index, which):
        if q < 2:
            return ref.at[q, index]
        return ref.at[q, index, pl.ds(0, 16) if which == 0 else pl.ds(16, 8)]

    def issue2(q, i, which):
        tile = lax.rem(me // 16 + i, 4)
        ssem = ssem2.at[q] if which == 0 else ssem3.at[0]
        rsem = rsem2.at[q, me // 4] if which == 0 else rsem3.at[0]

        def one(j, carry):
            dest = tile * 16 + lax.rem(me + j, 16)
            source, target = part(send2, q, dest, which), part(recv2, q, me, which)

            @pl.when(dest != me)
            def _():
                pltpu.make_async_remote_copy(
                    src_ref=source,
                    dst_ref=target,
                    send_sem=ssem,
                    recv_sem=rsem,
                    device_id={"ma": dest},
                    device_id_type=MESH,
                ).start()

            @pl.when(dest == me)
            def _():
                pltpu.make_async_copy(source, target, rsem).start()

            return carry

        lax.fori_loop(0, 16, one, 0)

    for q in range(3):
        span = recv1.at[q, pl.ds(0, PEERS - 1)]
        pltpu.make_async_copy(span, span, rsem1.at[q]).wait()
        pltpu.make_async_copy(recv1.at[q, 0], recv1.at[q, 0], lsem1.at[q]).wait()
        weight = quads[q : q + 1, :]

        def synthesise(i, carry):
            at = aligned(i * 256, 256)
            got = recv1[q].reshape(1024, 384)
            g = jnp.dot(synth[at, :], got, preferred_element_type=F32)
            c = [g[:, p * 128 : p * 128 + 128] for p in range(3)]
            r = [pltpu.roll(v, 64, 1) for v in c]
            d = []
            for a, b in ((1, 2), (2, 0), (0, 1)):
                t = c[a] * r[b]
                d.append(t - pltpu.roll(t, 64, 1))
            emf[at, 0:128] = (jnp.where(left_tall, d[1], -d[2]) * radius).astype(BF16)
            emf[at, 128:256] = d[0].astype(BF16)
            return carry

        lax.fori_loop(0, NLON // 256, synthesise, 0)

        def analyse(i, carry):
            tile = lax.rem(me // 16 + i, 4)
            w = jnp.dot(analysis[aligned(tile * 256, 256), :], emf[...], preferred_element_type=F32)
            dests = aligned(tile * 16, 16)
            send2[q, dests, 0:16, :] = (w[:, :128] * weight).reshape(16, 16, 128).astype(BF16)
            last = (w[:, 128:] * weight).reshape(16, 16, 128)
            lane3 = lax.broadcasted_iota(jnp.int32, (16, 8, 128), 2)
            pair = jnp.where(lane3 < 64, last[:, :8], -last[:, 8:])
            send2[q, dests, 16:24, :] = pair.astype(BF16)

            @pl.when(i > 0)
            def _():
                issue2(q, i - 1, 0)

            return carry

        lax.fori_loop(0, 4, analyse, 0)
        issue2(q, 3, 0)
        if q == 2:
            for i in range(4):
                issue2(q, i, 1)

    left8 = lax.broadcasted_iota(jnp.int32, (8, 128), 1) < 64

    def halos(q):
        up = pltpu.make_async_remote_copy(
            src_ref=recv2.at[q, pl.ds(60, 4), pl.ds(0, 16)],
            dst_ref=low.at[q],
            send_sem=hsend.at[2 * q],
            recv_sem=hrecv.at[2 * q],
            device_id={"row": above},
            device_id_type=MESH,
        )
        down = pltpu.make_async_remote_copy(
            src_ref=recv2.at[q, pl.ds(0, 4), pl.ds(0, 16)],
            dst_ref=high.at[q],
            send_sem=hsend.at[2 * q + 1],
            recv_sem=hrecv.at[2 * q + 1],
            device_id={"row": below},
            device_id_type=MESH,
        )
        return up, down

    def unpack(block, first, level):
        for pair in range(2):
            e, o = block(first + pair * 2), block(first + pair * 2 + 1)
            full[pair, aligned(level * 16, 16), :] = jnp.where(left, e, pltpu.roll(o, 64, 1))
            full[pair, aligned(288 + level * 16, 16), :] = jnp.where(left, pltpu.roll(e, 64, 1), o)

    puts = [
        pltpu.make_async_copy(
            coef.at[t, pl.ds(0, 768)], out_hbm.at[:, pl.ds(t * 128, 128)], in_sem.at[t]
        )
        for t in range(4)
    ]

    for q in range(3):
        up, down = halos(q)

        def own(n, carry):
            k = lax.rem(me // 16 + 4 - n // 4, 4) * 4 + lax.rem(n, 4)
            span = part(recv2, q, pl.ds(k * 4, 4), 0)
            pltpu.make_async_copy(span, span, rsem2.at[q, k]).wait()

            @pl.when(k == 15)
            def _():
                up.start()

            @pl.when(k == 0)
            def _():
                down.start()

            unpack(lambda i: recv2[q, i, 0:16, :].astype(F32), k * 4, k + 1)
            return carry

        lax.fori_loop(0, 16, own, 0)

        def derive(k, carry):
            index = row * 16 + k
            r = 0.5 + (jnp.full((16, 128), index.astype(F32), F32) + 0.5) * (1.0 / total)
            inv = 1.0 / r
            bottom, top = index == 0, index == total - 1
            hi = jnp.where(top, 0.0, jnp.where(bottom, 1.0, 0.5)) * inv
            mid = jnp.where(bottom, -1.0, jnp.where(top, 1.0, 0.0)) * inv
            lo = jnp.where(bottom, 0.0, jnp.where(top, -1.0, -0.5)) * inv
            for pair in range(2):

                def diff(at):
                    here = lambda n: full[pair, aligned(at + (k + n) * 16, 16), :]
                    return hi * here(2) + mid * here(1) + lo * here(0)

                lhs[pair, aligned(256 + k * 16, 16), :] = -diff(288)
                lhs[pair, aligned(512 + k * 16, 16), :] = diff(0)
            return carry

        lax.fori_loop(1, 15, derive, 0)
        up.wait_recv()
        down.wait_recv()
        unpack(lambda i: low[q, i].astype(F32), 0, 0)
        unpack(lambda i: high[q, i].astype(F32), 0, 17)
        derive(0, 0)
        derive(15, 0)

        if q == 2:
            span = part(recv2, q, pl.ds(0, PEERS), 1)
            pltpu.make_async_copy(span, span, rsem3.at[0]).wait()

        def radial(k, carry):
            for pair in range(2):
                e = recv2[q, k * 4 + pair * 2, 16:24, :].astype(F32)
                o = recv2[q, k * 4 + pair * 2 + 1, 16:24, :].astype(F32)
                lhs[pair, aligned(k * 16, 8), :] = jnp.where(left8, e, pltpu.roll(o, 64, 1))
                lhs[pair, aligned(k * 16 + 8, 8), :] = jnp.where(left8, pltpu.roll(e, 64, 1), o)
            return carry

        lax.fori_loop(0, 16, radial, 0)

        for half in range(2):
            lines = slice(half * 256, half * 256 + 256)
            for s in range(8):
                x = jnp.concatenate(
                    [lhs[0, pl.ds(s, 96, stride=8), :], lhs[1, pl.ds(s, 96, stride=8), :]], axis=1
                ).astype(BF16)
                table = jnp.concatenate(
                    [
                        leg[s, lines, q * 128 : q * 128 + 128],
                        leg[s, lines, q * 128 + 384 : q * 128 + 512],
                    ],
                    axis=1,
                )
                y = lax.dot_general(x, table, (((1,), (1,)), ((), ())), preferred_element_type=F32)
                if q > 0:
                    y = done[s, :, lines] + y
                if q < 2:
                    done[s, :, lines] = y
                else:
                    degree = lax.broadcasted_iota(jnp.int32, y.shape, 1) + half * 256
                    y = jnp.where(degree.astype(F32) >= small_ref[me * 8 + s], y, 0.0)
                    for t in range(2):
                        coef[half * 2 + t, pl.ds(s, 96, stride=8), :] = y[:, t * 128 : t * 128 + 128]
            if q == 2:
                for t in range(half * 2, half * 2 + 2):
                    puts[t].start()

    for q in range(3):
        span = send1.at[q, pl.ds(0, PEERS - 1)]
        pltpu.make_async_copy(span, span, ssem1.at[q]).wait()
        span = part(send2, q, pl.ds(0, PEERS - 1), 0)
        pltpu.make_async_copy(span, span, ssem2.at[q]).wait()
        if q == 2:
            span = part(send2, q, pl.ds(0, PEERS - 1), 1)
            pltpu.make_async_copy(span, span, ssem3.at[0]).wait()
        up, down = halos(q)
        up.wait_send()
        down.wait_send()
    for put in puts:
        put.wait()


def shards(fields, legendre, quad, assign):
    small = lax.pad(assign, jnp.int32(0), [(0, quad.shape[0], 0)]).astype(F32) + lax.pad(
        quad, F32(0), [(assign.shape[0], 0, 0)]
    )
    smem = pl.BlockSpec(memory_space=pltpu.SMEM)
    hbm = pl.BlockSpec(memory_space=pltpu.HBM)
    dma = pltpu.SemaphoreType.DMA
    result = pl.pallas_call(
        kernel,
        in_specs=[smem, hbm, hbm],
        out_specs=pl.BlockSpec(memory_space=pl.ANY),
        out_shape=jax.ShapeDtypeStruct((768, 512), F32),
        scratch_shapes=[
            pltpu.VMEM((1536, 512), BF16),
            pltpu.VMEM((4, 1536, 128), F32),
            pltpu.VMEM((8, 192, 512), BF16),
            pltpu.VMEM((8, 512, 768), BF16),
            pltpu.VMEM((2, 1536, 128), F32),
            pltpu.VMEM((3, PEERS, 16, 384), BF16),
            pltpu.VMEM((3, PEERS, 16, 384), BF16),
            pltpu.VMEM((NLON, 1024), BF16),
            pltpu.VMEM((1024, NLON), BF16),
            pltpu.VMEM((128, 1024), F32),
            pltpu.VMEM((128, 1024), F32),
            pltpu.VMEM((16, 1024), F32),
            pltpu.VMEM((16, 1024), F32),
            pltpu.VMEM((NLON, 256), BF16),
            pltpu.VMEM((3, PEERS, 24, 128), BF16),
            pltpu.VMEM((3, PEERS, 24, 128), BF16),
            pltpu.VMEM((3, 4, 16, 128), BF16),
            pltpu.VMEM((3, 4, 16, 128), BF16),
            pltpu.VMEM((2, 576, 128), F32),
            pltpu.VMEM((2, 768, 128), F32),
            pltpu.VMEM((8, 96, 512), F32),
            pltpu.VMEM((8, 1024), F32),
            pltpu.VMEM((8, 128), F32),
            dma((9,)),
            dma((3,)),
            dma((3,)),
            dma((3,)),
            dma((3,)),
            dma((3, 16)),
            dma((1,)),
            dma((1,)),
            dma((6,)),
            dma((6,)),
        ],
        compiler_params=pltpu.CompilerParams(
            collective_id=0, has_side_effects=True, vmem_limit_bytes=54_000_000
        ),
        name="induction",
    )(small, fields.reshape(1536, 512), legendre)
    return result.reshape(3, 16, 2, 8, 512)


def solution(mesh):
    return jax.shard_map(
        shards,
        mesh=mesh,
        in_specs=(P(None, "row", None, "ma", None), P("ma", None, None), P(), P()),
        out_specs=P(None, "row", None, "ma", None),
        check_vma=False,
    )
```
